32 devices in a mesh: section: 2 (over core), space: 16 (over z, y, x).
Axes of the slice: x: 2, y: 2, z: 4, core: 2. Of those that a mesh axis runs over, the one named last changes fastest.
Arguments:
- feats: bfloat16 [2, 384, 128, 128], P('section', 'space'), may hold values from -6 to 6
- w_first: bfloat16 [2, 27, 128, 128], P('section'), may hold values from -0.109375 to 0.109375
- w_second: bfloat16 [2, 27, 128, 128], P('section'), may hold values from -0.109375 to 0.109375
- w_skip: bfloat16 [27, 128, 128], replicated, may hold values from -0.109375 to 0.109375
- send_tiles: int32 [2, 128, 2], P('section', 'space'), may hold values from 0 to 23
- send_counts: int32 [2, 128], P('section', 'space'), may hold values from 0 to 2, as said below
- neighbours: int32 [2, 27, 384], P('section', None, 'space'), may hold values from 0 to 40, as said below
Outputs:
- outputs: bfloat16 [2, 384, 128, 128], P('section', 'space')
The draws below stay inside these ranges and needn't reach their ends.
Inputs may be any that keep to these rules, and one draw needn't show every extreme that they name: `send_tiles`: entry [s, p * 8 + d, j] names one of partition p's own tiles. `send_counts`: entry [s, p * 8 + d] is how many slots partition p fills toward its neighbour in direction d; 0 where that neighbour lies outside the grid. `neighbours`: for output tile t of partition q, a value below 24 is q's own tile, 24 + d * 2 + j is slot j of direction d in q's table, 40 is no neighbour; offset 13 names tile t itself.
All inputs are finite; a program needn't handle non-finite values.
Results may differ from the reference program's by a relative error of at most 0.0049.
Values may be sent and summed in bfloat16 or wider, within the bound.
A program may use at most 64 MiB of HBM per device.

```python
import math
import jax
import jax.numpy as jnp
from jax import lax

C = 128
VOX = 128
KOFF = 27
DIRS = 8
CAP = 2
GRID_B = 8
TILES = 24
GRID_A = 2
PARTITIONS = 16
TILES_ALL = 384
OUTBOX = 128
SLOTS = 16
EMPTY = 40


step_rows = (-1, -1, -1, 0, 0, 1, 1, 1)


step_cols = (-1, 0, 1, -1, 1, -1, 0, 1)


def draw_send_counts(key, part):
    partition = jnp.arange(PARTITIONS, dtype=jnp.int32)[:, None]
    grid_row = partition // GRID_B + jnp.array(step_rows, dtype=jnp.int32)[None, :]
    grid_col = partition % GRID_B + jnp.array(step_cols, dtype=jnp.int32)[None, :]
    inside = (grid_row >= 0) & (grid_row < GRID_A) & (grid_col >= 0) & (grid_col < GRID_B)
    counts = jax.random.randint(jax.random.fold_in(key, 11), (2, PARTITIONS, DIRS), 0, CAP + 1, dtype=jnp.int32)
    counts = jnp.where(inside[None], counts, 0)
    counts = counts.at[:, 0, 7].set(CAP)
    return counts.reshape(2, OUTBOX)


def draw_neighbours(key, part):
    full_shape = (2, KOFF, TILES_ALL)
    local_ids = jax.random.randint(jax.random.fold_in(key, 21), full_shape, 0, TILES, dtype=jnp.int32)
    remote_ids = jax.random.randint(jax.random.fold_in(key, 22), full_shape, TILES, EMPTY, dtype=jnp.int32)
    picker = jax.random.randint(jax.random.fold_in(key, 23), full_shape, 0, 20, dtype=jnp.int32)
    chosen = jnp.where(picker < 14, local_ids, jnp.where(picker < 19, remote_ids, EMPTY))
    centre = jnp.arange(TILES_ALL, dtype=jnp.int32) % TILES
    return chosen.at[:, 13, :].set(jnp.broadcast_to(centre, (2, TILES_ALL)))


def plant(values, rng, low, high):
    longest = values.shape.index(max(values.shape))
    spots = []
    for shift in (0, 1):
        where = [jax.random.randint(jax.random.fold_in(rng, axis), (), 0, length) for axis, length in enumerate(values.shape)]
        where[longest] = (where[longest] + shift) % values.shape[longest]
        spots.append(tuple(where))
    return values.at[spots[0]].set(low).at[spots[1]].set(high)


def shard_levels(own_key, shape, pieces, smallest, top_value):
    def one(dim, parts):
        heights = jax.random.uniform(jax.random.fold_in(jax.random.fold_in(own_key, 6), dim), (parts,), jnp.float32, smallest / len(pieces), top_value / len(pieces))
        return jnp.repeat(jnp.exp(heights), shape[dim] // parts).reshape((-1,) + (1,) * (len(shape) - dim - 1))

    loudness = one(*pieces[0])
    for cut in pieces[1:]:
        loudness = loudness * one(*cut)
    return loudness


def gaussian(rng, shape, spread, reach, split=(), held_as=jnp.bfloat16):
    factor_of = shard_levels(rng, shape, split, -0.22, 0.18) if split else 1.0
    drawn = jax.random.normal(rng, shape, jnp.float32) * spread * factor_of
    return jnp.minimum(jnp.maximum(drawn, -reach), reach).astype(held_as)


def setup_inputs(seed: int = 0) -> dict:
    keys = jax.random.split(jax.random.key(seed), 8)
    feats = gaussian(keys[0], (2, TILES_ALL, C, VOX), 1.0, 6.0, ((0, 2), (1, 16)))
    w_first = gaussian(keys[1], (2, KOFF, C, C), (KOFF * C) ** -0.5, 0.109375, ((0, 2),))
    w_second = gaussian(keys[2], (2, KOFF, C, C), (KOFF * C) ** -0.5, 0.109375, ((0, 2),))
    w_skip = gaussian(keys[3], (KOFF, C, C), (KOFF * C) ** -0.5, 0.109375)
    send_tiles = plant(jax.random.randint(keys[4], (2, OUTBOX, CAP), 0, TILES), jax.random.fold_in(keys[4], 1), 0, TILES - 1).astype(jnp.int32)
    send_counts = draw_send_counts(jax.random.fold_in(keys[7], 71), 0)
    neighbours = draw_neighbours(jax.random.fold_in(keys[7], 71), 0)
    return {"feats": feats, "w_first": w_first, "w_second": w_second, "w_skip": w_skip, "send_tiles": send_tiles, "send_counts": send_counts, "neighbours": neighbours}


step_rows = (-1, -1, -1, 0, 0, 1, 1, 1)
step_cols = (-1, 0, 1, -1, 1, -1, 0, 1)


def tile_conv(tile_table, tile_ids, weights):
    block_width = math.gcd(TILES, 8)
    grouped = tile_ids.T.reshape(TILES // block_width, block_width, KOFF)
    float_weights = weights.astype(jnp.float32)

    def one_block(block_ids):
        gathered = tile_table[block_ids].astype(jnp.float32)
        return jnp.einsum("koc,bkcv->bov", float_weights, gathered, precision=lax.Precision.HIGHEST)

    result = lax.map(one_block, grouped)
    return result.reshape(TILES, C, VOX)


def section_conv(tile_field, weights, send_rows, counts, tile_ids):
    rows_grid = send_rows.reshape(PARTITIONS, DIRS, CAP)
    count_grid = counts.reshape(PARTITIONS, DIRS)
    step_a = jnp.array(step_rows, dtype=jnp.int32)
    step_b = jnp.array(step_cols, dtype=jnp.int32)
    zero_tile = jnp.zeros((1,) + tile_field.shape[1:], tile_field.dtype)
    direction_ids = jnp.arange(DIRS, dtype=jnp.int32)

    def one_device(device):
        own_tiles = lax.dynamic_slice_in_dim(tile_field, device * TILES, TILES, 0)
        grid_row = device // GRID_B - step_a
        grid_col = device % GRID_B - step_b
        inside = (grid_row >= 0) & (grid_row < GRID_A) & (grid_col >= 0) & (grid_col < GRID_B)
        source = jnp.where(inside, grid_row * GRID_B + grid_col, 0).astype(jnp.int32)
        chosen = rows_grid[source, direction_ids]
        live_counts = jnp.where(inside, count_grid[source, direction_ids], 0)
        picked = tile_field[source[:, None] * TILES + chosen]
        live_slot = jnp.arange(CAP, dtype=jnp.int32)[None, :] < live_counts[:, None]
        picked = jnp.where(live_slot[:, :, None, None], picked, jnp.zeros_like(picked))
        tile_table = jnp.concatenate([own_tiles, picked.reshape((SLOTS,) + tile_field.shape[1:]), zero_tile], axis=0)
        local_ids = lax.dynamic_slice_in_dim(tile_ids, device * TILES, TILES, 1)
        return tile_conv(tile_table, local_ids, weights)

    result = lax.map(one_device, jnp.arange(PARTITIONS, dtype=jnp.int32))
    return result.reshape(TILES_ALL, C, VOX)


def reference(feats, w_first, w_second, w_skip, send_tiles, send_counts, neighbours):
    encoder_first = jax.nn.relu(section_conv(feats[0], w_first[0], send_tiles[0], send_counts[0], neighbours[0])).astype(jnp.bfloat16)
    decoder_first = jax.nn.relu(section_conv(feats[1], w_first[1], send_tiles[1], send_counts[1], neighbours[1])).astype(jnp.bfloat16)
    decoder_input = jnp.concatenate([decoder_first, encoder_first], axis=1)
    decoder_weights = jnp.concatenate([w_second[1], w_skip], axis=2)
    encoder_out = jax.nn.relu(section_conv(encoder_first, w_second[0], send_tiles[0], send_counts[0], neighbours[0])).astype(jnp.bfloat16)
    decoder_out = jax.nn.relu(section_conv(decoder_input, decoder_weights, send_tiles[1], send_counts[1], neighbours[1])).astype(jnp.bfloat16)
    return jnp.stack([encoder_out, decoder_out])
```

```python
import jax
import jax.numpy as jnp
from jax import lax
from jax.experimental import pallas as pl
from jax.experimental.pallas import tpu as pltpu
from jax.sharding import PartitionSpec as P

GRID_B = 8

step_rows = (-1, -1, -1, 0, 0, 1, 1, 1)
step_cols = (-1, 0, 1, -1, 1, -1, 0, 1)


def conv_pair(ids, w, table, first, second):
    koff = w.shape[0]
    acc = None
    for i in range(0, koff, 2):
        lhs, rhs = [], []
        for k in range(i, min(i + 2, koff)):
            lhs.append(w[k])
            rhs.append(jnp.concatenate([table[ids[first, k]], table[ids[second, k]]], axis=1))
        part = jnp.dot(
            jnp.concatenate(lhs, axis=1),
            jnp.concatenate(rhs, axis=0),
            preferred_element_type=jnp.float32,
        )
        acc = part if acc is None else acc + part
    return acc


def conv_tiles(ids, w, table, emit, tiles):
    width = 8 if tiles % 8 == 0 else 2

    def body(step, _):
        firsts = [step * width + i for i in range(0, width, 2)]
        parts = [conv_pair(ids, w, table, t, t + 1) for t in firsts]
        for t, part in zip(firsts, parts):
            emit(t, part)
        return 0

    lax.fori_loop(0, tiles // width, body, 0)


MESH = pl.DeviceIdType.MESH


def network(
    ids_hbm, rows_hbm, counts_hbm, feats, w1_hbm, w2_hbm, w3_hbm, out,
    ids, rows, counts,
    table1, table2, table3, w1, w2, w3, acc,
    outbox1, outbox2, outbox3, inbox1, inbox2, inbox3,
    local_sems, send1, recv1, send2, recv2, send3, recv3, send_skip, recv_skip, turn,
):
    tiles, _, vox = feats.shape
    cap, dirs = rows.shape
    across = [d for d in range(dirs) if step_rows[d] != 0]
    along = [d for d in range(dirs) if step_rows[d] == 0]
    section = lax.axis_index("section")
    me = lax.axis_index("space")
    grid_a = lax.axis_size("space") // GRID_B
    row, col = me // GRID_B, me % GRID_B

    def inside(d, sign):
        r, c = row + sign * step_rows[d], col + sign * step_cols[d]
        return (r >= 0) & (r < grid_a) & (c >= 0) & (c < GRID_B)

    def target(d):
        return {"section": section, "space": me + step_rows[d] * GRID_B + step_cols[d]}

    sibling = {"section": 1 - section, "space": me}

    barrier = pltpu.get_barrier_semaphore()
    for d in range(dirs):

        @pl.when(inside(d, 1))
        def _():
            pl.semaphore_signal(barrier, inc=1, device_id=target(d), device_id_type=MESH)

    pl.semaphore_signal(barrier, inc=1, device_id=sibling, device_id_type=MESH)

    loads = [
        pltpu.make_async_copy(src, dst, local_sems.at[i])
        for i, (src, dst) in enumerate(
            [
                (rows_hbm, rows),
                (counts_hbm, counts),
                (feats, table1.at[pl.ds(0, tiles)]),
                (ids_hbm, ids),
                (w1_hbm, w1),
                (w2_hbm, w2),
                (w3_hbm, w3),
            ]
        )
    ]
    for load in loads[:4]:
        load.start()

    def halo_copy(d, outbox, inbox, send, recv):
        return pltpu.make_async_remote_copy(
            src_ref=outbox.at[d],
            dst_ref=inbox.at[d],
            send_sem=send.at[d],
            recv_sem=recv.at[d],
            device_id=target(d),
            device_id_type=MESH,
        )

    def halo_fill(table, outbox):
        for d in across + along:
            for j in range(cap):
                tile = table[rows[j, d]]
                outbox[d, j] = jnp.where(j < counts[d], tile, jnp.zeros_like(tile))

    def halo_start(ds, outbox, inbox, send, recv):
        for d in ds:

            @pl.when(inside(d, 1))
            def _():
                halo_copy(d, outbox, inbox, send, recv).start()

    def halo_sent(ds, outbox, inbox, send, recv):
        for d in ds:

            @pl.when(inside(d, 1))
            def _():
                halo_copy(d, outbox, inbox, send, recv).wait_send()

    def halo_receive(table, outbox, inbox, send, recv):
        for d in range(dirs):
            place = pl.ds(tiles + d * cap, cap)

            @pl.when(inside(d, -1))
            def _():
                halo_copy(d, outbox, inbox, send, recv).wait_recv()
                table[place] = inbox[d]

            @pl.when(jnp.logical_not(inside(d, -1)))
            def _():
                table[place] = jnp.zeros((cap,) + table.shape[1:], table.dtype)

        table[tiles + dirs * cap] = jnp.zeros(table.shape[1:], table.dtype)

    def skip_copy(t):
        return pltpu.make_async_remote_copy(
            src_ref=table2.at[pl.ds(t, 2)],
            dst_ref=table3.at[pl.ds(t, 2)],
            send_sem=send_skip.at[t // 2],
            recv_sem=recv_skip.at[t // 2],
            device_id=sibling,
            device_id_type=MESH,
        )

    halo1 = (outbox1, inbox1, send1, recv1)
    halo2 = (outbox2, inbox2, send2, recv2)
    halo3 = (outbox3, inbox3, send3, recv3)

    for load in loads[:3]:
        load.wait()
    halo_fill(table1, outbox1)
    peers = jnp.int32(1)
    for d in range(dirs):
        peers += jnp.where(inside(d, -1), 1, 0).astype(jnp.int32)
    pl.semaphore_wait(barrier, peers)

    @pl.when(section == 0)
    def _():
        halo_start(across + along, *halo1)
        for load in loads[4:]:
            load.start()
        pl.semaphore_signal(turn, inc=1, device_id=sibling, device_id_type=MESH)
        halo_sent(across, *halo1)

    @pl.when(section == 1)
    def _():
        halo_start(along, *halo1)
        for load in loads[4:]:
            load.start()
        pl.semaphore_wait(turn, 1)
        halo_start(across, *halo1)

    loads[3].wait()
    loads[4].wait()
    halo_receive(table1, *halo1)

    def emit_first(t, part):
        part = jnp.maximum(part, 0.0).astype(table2.dtype)
        table2[t] = part[:, :vox]
        table2[t + 1] = part[:, vox:]

        @pl.when(section == 0)
        def _():
            skip_copy(t).start()

    def send_first(i, _):
        d = jnp.where(i < 3, i, jnp.where(i < 6, i + 2, i - 3)).astype(jnp.int32)
        step = d + jnp.where(d >= dirs // 2, 1, 0).astype(jnp.int32)
        da, db = step // 3 - 1, step % 3 - 1
        r, c = row + da, col + db

        @pl.when((r >= 0) & (r < grid_a) & (c >= 0) & (c < GRID_B))
        def _():
            part = conv_pair(ids, w1, table1, rows[0, d], rows[1, d])
            part = jnp.maximum(part, 0.0).astype(outbox2.dtype)
            for j in range(cap):
                tile = part[:, j * vox : (j + 1) * vox]
                outbox2[d, j] = jnp.where(j < counts[d], tile, jnp.zeros_like(tile))
            pltpu.make_async_remote_copy(
                src_ref=outbox2.at[d],
                dst_ref=inbox2.at[d],
                send_sem=send2.at[d],
                recv_sem=recv2.at[d],
                device_id={"section": section, "space": me + da * GRID_B + db},
                device_id_type=MESH,
            ).start()

        return 0

    lax.fori_loop(0, dirs, send_first, 0)
    conv_tiles(ids, w1, table1, emit_first, tiles)

    @pl.when(section == 1)
    def _():
        lax.fori_loop(0, tiles // 2, lambda i, _: (skip_copy(2 * i).wait_recv(), 0)[1], 0)
        halo_fill(table3, outbox3)
        halo_start(across + along, *halo3)

    for load in loads[5:]:
        load.wait()

    halo_receive(table2, *halo2)

    def emit_out(t, part):
        acc[t // 2] = part
        part = jnp.maximum(part, 0.0).astype(out.dtype)
        out[t] = part[:, :vox]
        out[t + 1] = part[:, vox:]

    conv_tiles(ids, w2, table2, emit_out, tiles)

    @pl.when(section == 1)
    def _():
        halo_receive(table3, *halo3)

        def emit_sum(t, part):
            part = jnp.maximum(part + acc[t // 2], 0.0).astype(out.dtype)
            out[t] = part[:, :vox]
            out[t + 1] = part[:, vox:]

        conv_tiles(ids, w3, table3, emit_sum, tiles)

    @pl.when(section == 0)
    def _():
        lax.fori_loop(0, tiles // 2, lambda i, _: (skip_copy(2 * i).wait_send(), 0)[1], 0)
        halo_sent(along, *halo1)

    @pl.when(section == 1)
    def _():
        halo_sent(across + along, *halo1)
        halo_sent(across + along, *halo3)

    halo_sent(across + along, *halo2)


def local(feats, w_first, w_second, w_skip, send_tiles, send_counts, neighbours):
    ids, send_rows, counts = neighbours[0], send_tiles[0], send_counts[0]
    own = feats[0]
    tiles, channels, vox = own.shape
    dirs, cap = send_rows.shape
    table = pltpu.VMEM((tiles + dirs * cap + 1, channels, vox), own.dtype)
    weights = pltpu.VMEM(w_skip.shape, w_skip.dtype)
    box = pltpu.VMEM((dirs, cap, channels, vox), own.dtype)
    anywhere = pl.BlockSpec(memory_space=pltpu.HBM)
    second = pl.pallas_call(
        network,
        out_shape=pltpu.VMEM((tiles, channels, vox), own.dtype),
        in_specs=[anywhere] * 7,
        out_specs=pl.BlockSpec(memory_space=pltpu.VMEM),
        scratch_shapes=[pltpu.SMEM(a.shape, a.dtype) for a in (ids.T, send_rows.T, counts)]
        + [table] * 3
        + [weights] * 3
        + [pltpu.VMEM((tiles // 2, channels, 2 * vox), jnp.float32)]
        + [box] * 6
        + [pltpu.SemaphoreType.DMA((7,))]
        + [pltpu.SemaphoreType.DMA((dirs,))] * 6
        + [pltpu.SemaphoreType.DMA((tiles // 2,))] * 2
        + [pltpu.SemaphoreType.REGULAR],
        compiler_params=pltpu.CompilerParams(
            collective_id=0, has_side_effects=True, vmem_limit_bytes=56 * 2**20
        ),
    )(ids.T, send_rows.T, counts, own, w_first[0], w_second[0], w_skip)
    return second[None]


def solution(mesh):
    placed = (
        P("section", "space", None, None),
        P("section", None, None, None),
        P("section", None, None, None),
        P(),
        P("section", "space", None),
        P("section", "space"),
        P("section", None, "space"),
    )
    return jax.shard_map(
        local,
        mesh=mesh,
        in_specs=placed,
        out_specs=P("section", "space", None, None),
        check_vma=False,
    )
```

```python
import jax
import jax.numpy as jnp
from jax import lax
from jax.experimental import pallas as pl
from jax.experimental.pallas import tpu as pltpu
from jax.sharding import PartitionSpec as P

GRID_B = 8

step_rows = (-1, -1, -1, 0, 0, 1, 1, 1)
step_cols = (-1, 0, 1, -1, 1, -1, 0, 1)


def conv_pair(ids, w, table, first, second):
    koff = w.shape[0]
    acc = None
    for i in range(0, koff, 2):
        lhs, rhs = [], []
        for k in range(i, min(i + 2, koff)):
            lhs.append(w[k])
            rhs.append(jnp.concatenate([table[ids[first, k]], table[ids[second, k]]], axis=1))
        part = jnp.dot(
            jnp.concatenate(lhs, axis=1),
            jnp.concatenate(rhs, axis=0),
            preferred_element_type=jnp.float32,
        )
        acc = part if acc is None else acc + part
    return acc


def conv_tiles(ids, w, table, emit, tiles, begin=0):
    width = 8 if tiles % 8 == 0 and begin % 8 == 0 else 2

    def body(step, _):
        firsts = [step * width + i for i in range(0, width, 2)]
        parts = [conv_pair(ids, w, table, t, t + 1) for t in firsts]
        for t, part in zip(firsts, parts):
            emit(t, part)
        return 0

    lax.fori_loop(begin // width, tiles // width, body, 0)


MESH = pl.DeviceIdType.MESH


def network(
    ids_hbm, rows_hbm, counts_hbm, feats, w1_hbm, w2_hbm, w3_hbm, out,
    ids, rows, counts,
    table1, table2, table3, w1, w2, w3, acc,
    outbox1, outbox2, outbox3, inbox1, inbox2, inbox3,
    local_sems, send1, recv1, send2, recv2, send3, recv3, send_skip, recv_skip,
    relay1, relay2, relay3, relay_send, relay_recv,
):
    tiles, _, vox = feats.shape
    cap, dirs = rows.shape
    corners = [d for d in range(dirs) if step_rows[d] != 0 and step_cols[d] != 0]
    across = corners + [d for d in range(dirs) if step_rows[d] != 0 and step_cols[d] == 0]
    along = [d for d in range(dirs) if step_rows[d] == 0]
    relays = (relay1, relay2, relay3)
    section = lax.axis_index("section")
    me = lax.axis_index("space")
    grid_a = lax.axis_size("space") // GRID_B
    row, col = me // GRID_B, me % GRID_B

    def inside(d, sign):
        r, c = row + sign * step_rows[d], col + sign * step_cols[d]
        return (r >= 0) & (r < grid_a) & (c >= 0) & (c < GRID_B)

    def target(d):
        return {"section": section, "space": me + step_rows[d] * GRID_B + step_cols[d]}

    sibling = {"section": 1 - section, "space": me}

    barrier = pltpu.get_barrier_semaphore()
    for d in range(dirs):

        @pl.when(inside(d, 1))
        def _():
            pl.semaphore_signal(barrier, inc=1, device_id=target(d), device_id_type=MESH)

    pl.semaphore_signal(barrier, inc=1, device_id=sibling, device_id_type=MESH)

    loads = [
        pltpu.make_async_copy(src, dst, local_sems.at[i])
        for i, (src, dst) in enumerate(
            [
                (rows_hbm, rows),
                (counts_hbm, counts),
                (feats, table1.at[pl.ds(0, tiles)]),
                (ids_hbm, ids),
                (w1_hbm, w1),
                (w2_hbm, w2),
                (w3_hbm, w3),
            ]
        )
    ]
    for load in loads[:4]:
        load.start()

    def halo_copy(d, outbox, inbox, send, recv):
        return pltpu.make_async_remote_copy(
            src_ref=outbox.at[d],
            dst_ref=inbox.at[d],
            send_sem=send.at[d],
            recv_sem=recv.at[d],
            device_id=target(d),
            device_id_type=MESH,
        )

    def halo_fill(table, outbox):
        for d in across + along:
            for j in range(cap):
                tile = table[rows[j, d]]
                outbox[d, j] = jnp.where(j < counts[d], tile, jnp.zeros_like(tile))

    def outer(d, at):
        edge = at if step_cols[d] < 0 else GRID_B - 1 - at
        return col == edge

    def relay_in(u, d, outbox):
        v = (step_rows[d] + 1) // 2
        return pltpu.make_async_remote_copy(
            src_ref=outbox.at[d, cap - 1],
            dst_ref=relays[u].at[v],
            send_sem=relay_send.at[u, v],
            recv_sem=relay_recv.at[u, v],
            device_id={"section": section, "space": me + step_cols[d]},
            device_id_type=MESH,
        )

    def relay_out(u, d, inbox, recv):
        v = (step_rows[d] + 1) // 2
        return pltpu.make_async_remote_copy(
            src_ref=relays[u].at[v],
            dst_ref=inbox.at[d, cap - 1],
            send_sem=relay_send.at[u, v],
            recv_sem=recv.at[d],
            device_id={"section": section, "space": me + step_rows[d] * GRID_B},
            device_id_type=MESH,
        )

    def direct(d, outbox, inbox, send, recv):
        return pltpu.make_async_remote_copy(
            src_ref=outbox.at[d, pl.ds(0, cap - 1)],
            dst_ref=inbox.at[d, pl.ds(0, cap - 1)],
            send_sem=send.at[d],
            recv_sem=recv.at[d],
            device_id=target(d),
            device_id_type=MESH,
        )

    def relaying(d):
        r = row + step_rows[d]
        return outer(d, 0) & (r >= 0) & (r < grid_a)

    def relay_forward(u, outbox, inbox, send, recv):
        for d in corners:

            @pl.when(relaying(d))
            def _():
                relay_in(u, d, outbox).wait_recv()
                relay_out(u, d, inbox, recv).start()

    def relay_sent(u, outbox, inbox, send, recv):
        for d in corners:

            @pl.when(relaying(d))
            def _():
                relay_out(u, d, inbox, recv).wait_send()

    def halo_start(u, ds, outbox, inbox, send, recv):
        for d in ds:
            if d in corners:

                @pl.when(inside(d, 1) & outer(d, 1) & (u < 2))
                def _():
                    relay_in(u, d, outbox).start()
                    direct(d, outbox, inbox, send, recv).start()

                @pl.when(inside(d, 1) & jnp.logical_not(outer(d, 1) & (u < 2)))
                def _():
                    halo_copy(d, outbox, inbox, send, recv).start()

            else:

                @pl.when(inside(d, 1))
                def _():
                    halo_copy(d, outbox, inbox, send, recv).start()

    def halo_sent(u, ds, outbox, inbox, send, recv):
        for d in ds:
            if d in corners:

                @pl.when(inside(d, 1) & outer(d, 1) & (u < 2))
                def _():
                    relay_in(u, d, outbox).wait_send()
                    direct(d, outbox, inbox, send, recv).wait_send()

                @pl.when(inside(d, 1) & jnp.logical_not(outer(d, 1) & (u < 2)))
                def _():
                    halo_copy(d, outbox, inbox, send, recv).wait_send()

            else:

                @pl.when(inside(d, 1))
                def _():
                    halo_copy(d, outbox, inbox, send, recv).wait_send()

    def halo_receive(table, outbox, inbox, send, recv):
        for d in range(dirs):
            place = pl.ds(tiles + d * cap, cap)

            @pl.when(inside(d, -1))
            def _():
                halo_copy(d, outbox, inbox, send, recv).wait_recv()
                table[place] = inbox[d]

            @pl.when(jnp.logical_not(inside(d, -1)))
            def _():
                table[place] = jnp.zeros((cap,) + table.shape[1:], table.dtype)

        table[tiles + dirs * cap] = jnp.zeros(table.shape[1:], table.dtype)

    def skip_copy(t):
        return pltpu.make_async_remote_copy(
            src_ref=table2.at[pl.ds(t, 2)],
            dst_ref=table3.at[pl.ds(t, 2)],
            send_sem=send_skip.at[t // 2],
            recv_sem=recv_skip.at[t // 2],
            device_id=sibling,
            device_id_type=MESH,
        )

    halo1 = (outbox1, inbox1, send1, recv1)
    halo2 = (outbox2, inbox2, send2, recv2)
    halo3 = (outbox3, inbox3, send3, recv3)

    for load in loads[:3]:
        load.wait()
    halo_fill(table1, outbox1)
    peers = jnp.int32(1)
    for d in range(dirs):
        peers += jnp.where(inside(d, -1), 1, 0).astype(jnp.int32)
    pl.semaphore_wait(barrier, peers)

    halo_start(0, across + along, *halo1)
    for load in loads[4:]:
        load.start()
    relay_forward(0, *halo1)

    loads[3].wait()
    loads[4].wait()
    halo_receive(table1, *halo1)

    def emit_first(t, part):
        part = jnp.maximum(part, 0.0).astype(table2.dtype)
        table2[t] = part[:, :vox]
        table2[t + 1] = part[:, vox:]

        @pl.when(section == 0)
        def _():
            skip_copy(t).start()

    def send_first(i, _):
        d = jnp.where(i < 4, 2 * i + i // 2, jnp.where(i < 6, 5 * i - 19, i - 3)).astype(jnp.int32)
        step = d + jnp.where(d >= dirs // 2, 1, 0).astype(jnp.int32)
        da, db = step // 3 - 1, step % 3 - 1
        r, c = row + da, col + db

        @pl.when((r >= 0) & (r < grid_a) & (c >= 0) & (c < GRID_B))
        def _():
            part = conv_pair(ids, w1, table1, rows[0, d], rows[1, d])
            part = jnp.maximum(part, 0.0).astype(outbox2.dtype)
            for j in range(cap):
                tile = part[:, j * vox : (j + 1) * vox]
                outbox2[d, j] = jnp.where(j < counts[d], tile, jnp.zeros_like(tile))
            far = {"section": section, "space": me + da * GRID_B + db}
            via = (da != 0) & (((db < 0) & (col == 1)) | ((db > 0) & (col == GRID_B - 2)))
            v = (da + 1) // 2

            @pl.when(via)
            def _():
                pltpu.make_async_remote_copy(
                    src_ref=outbox2.at[d, cap - 1],
                    dst_ref=relay2.at[v],
                    send_sem=relay_send.at[1, v],
                    recv_sem=relay_recv.at[1, v],
                    device_id={"section": section, "space": me + db},
                    device_id_type=MESH,
                ).start()
                pltpu.make_async_remote_copy(
                    src_ref=outbox2.at[d, pl.ds(0, cap - 1)],
                    dst_ref=inbox2.at[d, pl.ds(0, cap - 1)],
                    send_sem=send2.at[d],
                    recv_sem=recv2.at[d],
                    device_id=far,
                    device_id_type=MESH,
                ).start()

            @pl.when(jnp.logical_not(via))
            def _():
                pltpu.make_async_remote_copy(
                    src_ref=outbox2.at[d],
                    dst_ref=inbox2.at[d],
                    send_sem=send2.at[d],
                    recv_sem=recv2.at[d],
                    device_id=far,
                    device_id_type=MESH,
                ).start()

        return 0

    lax.fori_loop(0, dirs, send_first, 0)
    conv_tiles(ids, w1, table1, emit_first, tiles // 3)
    relay_forward(1, *halo2)
    conv_tiles(ids, w1, table1, emit_first, tiles, tiles // 3)

    @pl.when(section == 1)
    def _():
        lax.fori_loop(0, tiles // 2, lambda i, _: (skip_copy(2 * i).wait_recv(), 0)[1], 0)
        halo_fill(table3, outbox3)
        halo_start(2, across + along, *halo3)

    for load in loads[5:]:
        load.wait()

    halo_receive(table2, *halo2)

    def emit_out(t, part):
        acc[t // 2] = part
        part = jnp.maximum(part, 0.0).astype(out.dtype)
        out[t] = part[:, :vox]
        out[t + 1] = part[:, vox:]

    conv_tiles(ids, w2, table2, emit_out, tiles)

    @pl.when(section == 1)
    def _():
        halo_receive(table3, *halo3)

        def emit_sum(t, part):
            part = jnp.maximum(part + acc[t // 2], 0.0).astype(out.dtype)
            out[t] = part[:, :vox]
            out[t + 1] = part[:, vox:]

        conv_tiles(ids, w3, table3, emit_sum, tiles)

    @pl.when(section == 0)
    def _():
        lax.fori_loop(0, tiles // 2, lambda i, _: (skip_copy(2 * i).wait_send(), 0)[1], 0)

    @pl.when(section == 1)
    def _():
        halo_sent(2, across + along, *halo3)

    halo_sent(0, across + along, *halo1)
    halo_sent(1, across + along, *halo2)
    relay_sent(0, *halo1)
    relay_sent(1, *halo2)


def local(feats, w_first, w_second, w_skip, send_tiles, send_counts, neighbours):
    ids, send_rows, counts = neighbours[0], send_tiles[0], send_counts[0]
    own = feats[0]
    tiles, channels, vox = own.shape
    dirs, cap = send_rows.shape
    table = pltpu.VMEM((tiles + dirs * cap + 1, channels, vox), own.dtype)
    weights = pltpu.VMEM(w_skip.shape, w_skip.dtype)
    box = pltpu.VMEM((dirs, cap, channels, vox), own.dtype)
    anywhere = pl.BlockSpec(memory_space=pltpu.HBM)
    second = pl.pallas_call(
        network,
        out_shape=pltpu.VMEM((tiles, channels, vox), own.dtype),
        in_specs=[anywhere] * 7,
        out_specs=pl.BlockSpec(memory_space=pltpu.VMEM),
        scratch_shapes=[pltpu.SMEM(a.shape, a.dtype) for a in (ids.T, send_rows.T, counts)]
        + [table] * 3
        + [weights] * 3
        + [pltpu.VMEM((tiles // 2, channels, 2 * vox), jnp.float32)]
        + [box] * 6
        + [pltpu.SemaphoreType.DMA((7,))]
        + [pltpu.SemaphoreType.DMA((dirs,))] * 6
        + [pltpu.SemaphoreType.DMA((tiles // 2,))] * 2
        + [pltpu.VMEM((2, channels, vox), own.dtype)] * 3
        + [pltpu.SemaphoreType.DMA((3, 2))] * 2,
        compiler_params=pltpu.CompilerParams(
            collective_id=0, has_side_effects=True, vmem_limit_bytes=56 * 2**20
        ),
    )(ids.T, send_rows.T, counts, own, w_first[0], w_second[0], w_skip)
    return second[None]


def solution(mesh):
    placed = (
        P("section", "space", None, None),
        P("section", None, None, None),
        P("section", None, None, None),
        P(),
        P("section", "space", None),
        P("section", "space"),
        P("section", None, "space"),
    )
    return jax.shard_map(
        local,
        mesh=mesh,
        in_specs=placed,
        out_specs=P("section", "space", None, None),
        check_vma=False,
    )
```

```python
import jax
import jax.numpy as jnp
from jax import lax
from jax.experimental import pallas as pl
from jax.experimental.pallas import tpu as pltpu
from jax.sharding import PartitionSpec as P

GRID_B = 8

step_rows = (-1, -1, -1, 0, 0, 1, 1, 1)
step_cols = (-1, 0, 1, -1, 1, -1, 0, 1)


def conv_pair(ids, w, table, first, second):
    koff = w.shape[0]
    acc = None
    for i in range(0, koff, 2):
        lhs, rhs = [], []
        for k in range(i, min(i + 2, koff)):
            lhs.append(w[k])
            rhs.append(jnp.concatenate([table[ids[first, k]], table[ids[second, k]]], axis=1))
        part = jnp.dot(
            jnp.concatenate(lhs, axis=1),
            jnp.concatenate(rhs, axis=0),
            preferred_element_type=jnp.float32,
        )
        acc = part if acc is None else acc + part
    return acc


def conv_tiles(ids, w, table, emit, begin, end, width):
    def body(step, _):
        firsts = [begin + step * width + i for i in range(0, width, 2)]
        parts = [conv_pair(ids, w, table, t, t + 1) for t in firsts]
        for t, part in zip(firsts, parts):
            emit(t, part)
        return 0

    if end - begin == width:
        body(0, 0)
    else:
        lax.fori_loop(0, (end - begin) // width, body, 0)


MESH = pl.DeviceIdType.MESH


def network(
    ids_hbm, rows_hbm, counts_hbm, feats, w1_hbm, w2_hbm, w3_hbm, out,
    ids, rows, counts,
    table1, table2, table3, w1, w2, w3, acc,
    outbox1, outbox2, outbox3, inbox1, inbox2, inbox3,
    local_sems, send1, recv1, send2, recv2, send3, recv3, send_skip, recv_skip,
    relay1, relay2, relay3, relay_send, relay_recv,
):
    tiles, _, vox = feats.shape
    cap, dirs = rows.shape
    corners = [d for d in range(dirs) if step_rows[d] != 0 and step_cols[d] != 0]
    across = corners + [d for d in range(dirs) if step_rows[d] != 0 and step_cols[d] == 0]
    along = [d for d in range(dirs) if step_rows[d] == 0]
    relays = (relay1, relay2, relay3)
    section = lax.axis_index("section")
    me = lax.axis_index("space")
    grid_a = lax.axis_size("space") // GRID_B
    row, col = me // GRID_B, me % GRID_B

    def inside(d, sign):
        r, c = row + sign * step_rows[d], col + sign * step_cols[d]
        return (r >= 0) & (r < grid_a) & (c >= 0) & (c < GRID_B)

    def target(d):
        return {"section": section, "space": me + step_rows[d] * GRID_B + step_cols[d]}

    sibling = {"section": 1 - section, "space": me}

    barrier = pltpu.get_barrier_semaphore()
    for d in range(dirs):

        @pl.when(inside(d, 1))
        def _():
            pl.semaphore_signal(barrier, inc=1, device_id=target(d), device_id_type=MESH)

    pl.semaphore_signal(barrier, inc=1, device_id=sibling, device_id_type=MESH)

    loads = [
        pltpu.make_async_copy(src, dst, local_sems.at[i])
        for i, (src, dst) in enumerate(
            [
                (feats, table1.at[pl.ds(0, tiles)]),
                (rows_hbm, rows),
                (counts_hbm, counts),
                (ids_hbm, ids),
                (w1_hbm, w1),
                (w2_hbm, w2),
                (w3_hbm, w3),
            ]
        )
    ]
    for load in loads[:4]:
        load.start()

    def halo_copy(d, outbox, inbox, send, recv):
        return pltpu.make_async_remote_copy(
            src_ref=outbox.at[d],
            dst_ref=inbox.at[d],
            send_sem=send.at[d],
            recv_sem=recv.at[d],
            device_id=target(d),
            device_id_type=MESH,
        )

    def outer(d, at):
        edge = at if step_cols[d] < 0 else GRID_B - 1 - at
        return col == edge

    def relay_in(u, d, outbox):
        v = (step_rows[d] + 1) // 2
        return pltpu.make_async_remote_copy(
            src_ref=outbox.at[d, cap - 1],
            dst_ref=relays[u].at[v],
            send_sem=relay_send.at[u, v],
            recv_sem=relay_recv.at[u, v],
            device_id={"section": section, "space": me + step_cols[d]},
            device_id_type=MESH,
        )

    def relay_out(u, d, inbox, recv):
        v = (step_rows[d] + 1) // 2
        return pltpu.make_async_remote_copy(
            src_ref=relays[u].at[v],
            dst_ref=inbox.at[d, cap - 1],
            send_sem=relay_send.at[u, v],
            recv_sem=recv.at[d],
            device_id={"section": section, "space": me + step_rows[d] * GRID_B},
            device_id_type=MESH,
        )

    def direct(d, outbox, inbox, send, recv):
        return pltpu.make_async_remote_copy(
            src_ref=outbox.at[d, pl.ds(0, cap - 1)],
            dst_ref=inbox.at[d, pl.ds(0, cap - 1)],
            send_sem=send.at[d],
            recv_sem=recv.at[d],
            device_id=target(d),
            device_id_type=MESH,
        )

    def relaying(d):
        r = row + step_rows[d]
        return outer(d, 0) & (r >= 0) & (r < grid_a)

    def relay_forward(u, outbox, inbox, send, recv):
        for d in corners:

            @pl.when(relaying(d))
            def _():
                relay_in(u, d, outbox).wait_recv()
                relay_out(u, d, inbox, recv).start()

    def relay_sent(u, outbox, inbox, send, recv):
        for d in corners:

            @pl.when(relaying(d))
            def _():
                relay_out(u, d, inbox, recv).wait_send()

    def halo_start(u, ds, table, outbox, inbox, send, recv):
        for d in ds:

            @pl.when(inside(d, 1))
            def _():
                for j in range(cap):
                    tile = table[rows[j, d]]
                    outbox[d, j] = jnp.where(j < counts[d], tile, jnp.zeros_like(tile))
                if d in corners:

                    @pl.when(outer(d, 1) & (u < 2))
                    def _():
                        relay_in(u, d, outbox).start()
                        direct(d, outbox, inbox, send, recv).start()

                    @pl.when(jnp.logical_not(outer(d, 1) & (u < 2)))
                    def _():
                        halo_copy(d, outbox, inbox, send, recv).start()

                else:
                    halo_copy(d, outbox, inbox, send, recv).start()

    def halo_sent(u, ds, outbox, inbox, send, recv):
        for d in ds:
            if d in corners:

                @pl.when(inside(d, 1) & outer(d, 1) & (u < 2))
                def _():
                    relay_in(u, d, outbox).wait_send()
                    direct(d, outbox, inbox, send, recv).wait_send()

                @pl.when(inside(d, 1) & jnp.logical_not(outer(d, 1) & (u < 2)))
                def _():
                    halo_copy(d, outbox, inbox, send, recv).wait_send()

            else:

                @pl.when(inside(d, 1))
                def _():
                    halo_copy(d, outbox, inbox, send, recv).wait_send()

    def halo_receive(table, outbox, inbox, send, recv):
        for d in range(dirs):
            place = pl.ds(tiles + d * cap, cap)

            @pl.when(inside(d, -1))
            def _():
                halo_copy(d, outbox, inbox, send, recv).wait_recv()
                table[place] = inbox[d]

            @pl.when(jnp.logical_not(inside(d, -1)))
            def _():
                table[place] = jnp.zeros((cap,) + table.shape[1:], table.dtype)

        table[tiles + dirs * cap] = jnp.zeros(table.shape[1:], table.dtype)

    def skip_copy(t):
        return pltpu.make_async_remote_copy(
            src_ref=table2.at[pl.ds(t, 2)],
            dst_ref=table3.at[pl.ds(t, 2)],
            send_sem=send_skip.at[t // 2],
            recv_sem=recv_skip.at[t // 2],
            device_id=sibling,
            device_id_type=MESH,
        )

    halo1 = (outbox1, inbox1, send1, recv1)
    halo2 = (outbox2, inbox2, send2, recv2)
    halo3 = (outbox3, inbox3, send3, recv3)

    for load in loads[:3]:
        load.wait()
    peers = jnp.int32(1)
    for d in range(dirs):
        peers += jnp.where(inside(d, -1), 1, 0).astype(jnp.int32)
    pl.semaphore_wait(barrier, peers)

    halo_start(0, across + along, table1, *halo1)
    for load in loads[4:]:
        load.start()
    relay_forward(0, *halo1)

    loads[3].wait()
    loads[4].wait()
    halo_receive(table1, *halo1)

    def emit_first(t, part):
        part = jnp.maximum(part, 0.0).astype(table2.dtype)
        table2[t] = part[:, :vox]
        table2[t + 1] = part[:, vox:]

        @pl.when(section == 0)
        def _():
            skip_copy(t).start()

    def send_first(i, _):
        d = jnp.where(i < 4, 2 * i + i // 2, jnp.where(i < 6, 5 * i - 19, i - 3)).astype(jnp.int32)
        step = d + jnp.where(d >= dirs // 2, 1, 0).astype(jnp.int32)
        da, db = step // 3 - 1, step % 3 - 1
        r, c = row + da, col + db

        @pl.when((r >= 0) & (r < grid_a) & (c >= 0) & (c < GRID_B))
        def _():
            part = conv_pair(ids, w1, table1, rows[0, d], rows[1, d])
            part = jnp.maximum(part, 0.0).astype(outbox2.dtype)
            for j in range(cap):
                tile = part[:, j * vox : (j + 1) * vox]
                outbox2[d, j] = jnp.where(j < counts[d], tile, jnp.zeros_like(tile))
            far = {"section": section, "space": me + da * GRID_B + db}
            via = (da != 0) & (((db < 0) & (col == 1)) | ((db > 0) & (col == GRID_B - 2)))
            v = (da + 1) // 2

            @pl.when(via)
            def _():
                pltpu.make_async_remote_copy(
                    src_ref=outbox2.at[d, cap - 1],
                    dst_ref=relay2.at[v],
                    send_sem=relay_send.at[1, v],
                    recv_sem=relay_recv.at[1, v],
                    device_id={"section": section, "space": me + db},
                    device_id_type=MESH,
                ).start()
                pltpu.make_async_remote_copy(
                    src_ref=outbox2.at[d, pl.ds(0, cap - 1)],
                    dst_ref=inbox2.at[d, pl.ds(0, cap - 1)],
                    send_sem=send2.at[d],
                    recv_sem=recv2.at[d],
                    device_id=far,
                    device_id_type=MESH,
                ).start()

            @pl.when(jnp.logical_not(via))
            def _():
                pltpu.make_async_remote_copy(
                    src_ref=outbox2.at[d],
                    dst_ref=inbox2.at[d],
                    send_sem=send2.at[d],
                    recv_sem=recv2.at[d],
                    device_id=far,
                    device_id_type=MESH,
                ).start()

        return 0

    lax.fori_loop(0, dirs, send_first, 0)
    conv_tiles(ids, w1, table1, emit_first, 0, tiles // 3, tiles // 3)
    relay_forward(1, *halo2)
    conv_tiles(ids, w1, table1, emit_first, tiles // 3, tiles, tiles // 3)

    @pl.when(section == 1)
    def _():
        lax.fori_loop(0, tiles // 2, lambda i, _: (skip_copy(2 * i).wait_recv(), 0)[1], 0)
        halo_start(2, across + along, table3, *halo3)

    for load in loads[5:]:
        load.wait()

    halo_receive(table2, *halo2)

    def emit_out(t, part):
        acc[t // 2] = part
        part = jnp.maximum(part, 0.0).astype(out.dtype)
        out[t] = part[:, :vox]
        out[t + 1] = part[:, vox:]

    conv_tiles(ids, w2, table2, emit_out, 0, tiles, tiles)

    @pl.when(section == 1)
    def _():
        halo_receive(table3, *halo3)

        def emit_sum(t, part):
            part = jnp.maximum(part + acc[t // 2], 0.0).astype(out.dtype)
            out[t] = part[:, :vox]
            out[t + 1] = part[:, vox:]

        conv_tiles(ids, w3, table3, emit_sum, 0, tiles, tiles)

    @pl.when(section == 0)
    def _():
        lax.fori_loop(0, tiles // 2, lambda i, _: (skip_copy(2 * i).wait_send(), 0)[1], 0)

    @pl.when(section == 1)
    def _():
        halo_sent(2, across + along, *halo3)

    halo_sent(0, across + along, *halo1)
    halo_sent(1, across + along, *halo2)
    relay_sent(0, *halo1)
    relay_sent(1, *halo2)


def local(feats, w_first, w_second, w_skip, send_tiles, send_counts, neighbours):
    ids, send_rows, counts = neighbours[0], send_tiles[0], send_counts[0]
    own = feats[0]
    tiles, channels, vox = own.shape
    dirs, cap = send_rows.shape
    table = pltpu.VMEM((tiles + dirs * cap + 1, channels, vox), own.dtype)
    weights = pltpu.VMEM(w_skip.shape, w_skip.dtype)
    box = pltpu.VMEM((dirs, cap, channels, vox), own.dtype)
    anywhere = pl.BlockSpec(memory_space=pltpu.HBM)
    second = pl.pallas_call(
        network,
        out_shape=pltpu.VMEM((tiles, channels, vox), own.dtype),
        in_specs=[anywhere] * 7,
        out_specs=pl.BlockSpec(memory_space=pltpu.VMEM),
        scratch_shapes=[pltpu.SMEM(a.shape, a.dtype) for a in (ids.T, send_rows.T, counts)]
        + [table] * 3
        + [weights] * 3
        + [pltpu.VMEM((tiles // 2, channels, 2 * vox), jnp.float32)]
        + [box] * 6
        + [pltpu.SemaphoreType.DMA((7,))]
        + [pltpu.SemaphoreType.DMA((dirs,))] * 6
        + [pltpu.SemaphoreType.DMA((tiles // 2,))] * 2
        + [pltpu.VMEM((2, channels, vox), own.dtype)] * 3
        + [pltpu.SemaphoreType.DMA((3, 2))] * 2,
        compiler_params=pltpu.CompilerParams(
            collective_id=0, has_side_effects=True, vmem_limit_bytes=56 * 2**20
        ),
    )(ids.T, send_rows.T, counts, own, w_first[0], w_second[0], w_skip)
    return second[None]


def solution(mesh):
    placed = (
        P("section", "space", None, None),
        P("section", None, None, None),
        P("section", None, None, None),
        P(),
        P("section", "space", None),
        P("section", "space"),
        P("section", None, "space"),
    )
    return jax.shard_map(
        local,
        mesh=mesh,
        in_specs=placed,
        out_specs=P("section", "space", None, None),
        check_vma=False,
    )
```

```python
import jax
import jax.numpy as jnp
from jax import lax
from jax.experimental import pallas as pl
from jax.experimental.pallas import tpu as pltpu
from jax.sharding import PartitionSpec as P

GRID_B = 8

step_rows = (-1, -1, -1, 0, 0, 1, 1, 1)
step_cols = (-1, 0, 1, -1, 1, -1, 0, 1)


def gather_pair(ids, table, k, first, second):
    return jnp.concatenate([table[ids[first, k]], table[ids[second, k]]], axis=1)


def conv_pair(ids, w, table, first, second, offsets=None, more=None):
    offsets = list(range(w.shape[0])) if offsets is None else offsets
    terms = [(w, table, k) for k in offsets] + ([] if more is None else [more])
    acc = None
    for i in range(0, len(terms), 2):
        lhs = [weight[k] for weight, _, k in terms[i : i + 2]]
        rhs = [
            jnp.concatenate([source[first], source[second]], axis=1)
            if more is not None and source is more[1]
            else gather_pair(ids, source, k, first, second)
            for _, source, k in terms[i : i + 2]
        ]
        part = jnp.dot(
            jnp.concatenate(lhs, axis=1),
            jnp.concatenate(rhs, axis=0),
            preferred_element_type=jnp.float32,
        )
        acc = part if acc is None else acc + part
    return acc


def conv_tiles(ids, w, table, emit, begin, end, width, offsets=None, more=None):
    def body(step, _):
        firsts = [begin + step * width + i for i in range(0, width, 2)]
        parts = [conv_pair(ids, w, table, t, t + 1, offsets, more) for t in firsts]
        for t, part in zip(firsts, parts):
            emit(t, part)
        return 0

    if end - begin == width:
        body(0, 0)
    else:
        lax.fori_loop(0, (end - begin) // width, body, 0)


MESH = pl.DeviceIdType.MESH


def network(
    ids_hbm, rows_hbm, counts_hbm, feats, w1_hbm, w2_hbm, w3_hbm, out,
    ids, rows, counts,
    table1, table2, table3, w1, w2, w3, acc,
    outbox1, outbox2, outbox3, inbox1, inbox2, inbox3,
    local_sems, send1, recv1, send2, recv2, send3, recv3, send_skip, recv_skip,
    relay1, relay2, relay3, relay_send, relay_recv,
):
    tiles, _, vox = feats.shape
    cap, dirs = rows.shape
    koff = w1.shape[0]
    outer_offsets = [k for k in range(koff) if k != koff // 2]
    corners = [d for d in range(dirs) if step_rows[d] != 0 and step_cols[d] != 0]
    order = [0, 2, 5, 7, 3, 4, 1, 6]
    relays = (relay1, relay2, relay3)
    section = lax.axis_index("section")
    me = lax.axis_index("space")
    grid_a = lax.axis_size("space") // GRID_B
    row, col = me // GRID_B, me % GRID_B

    def inside(d, sign):
        r, c = row + sign * step_rows[d], col + sign * step_cols[d]
        return (r >= 0) & (r < grid_a) & (c >= 0) & (c < GRID_B)

    def target(d):
        return {"section": section, "space": me + step_rows[d] * GRID_B + step_cols[d]}

    sibling = {"section": 1 - section, "space": me}

    barrier = pltpu.get_barrier_semaphore()
    for d in range(dirs):

        @pl.when(inside(d, 1))
        def _():
            pl.semaphore_signal(barrier, inc=1, device_id=target(d), device_id_type=MESH)

    pl.semaphore_signal(barrier, inc=1, device_id=sibling, device_id_type=MESH)

    loads = [
        pltpu.make_async_copy(src, dst, local_sems.at[i])
        for i, (src, dst) in enumerate(
            [
                (feats, table1.at[pl.ds(0, tiles)]),
                (rows_hbm, rows),
                (counts_hbm, counts),
                (ids_hbm, ids),
                (w1_hbm, w1),
                (w2_hbm, w2),
                (w3_hbm, w3),
            ]
        )
    ]
    for load in loads[:4]:
        load.start()

    def halo_copy(d, outbox, inbox, send, recv):
        return pltpu.make_async_remote_copy(
            src_ref=outbox.at[d],
            dst_ref=inbox.at[d],
            send_sem=send.at[d],
            recv_sem=recv.at[d],
            device_id=target(d),
            device_id_type=MESH,
        )

    def outer(d, at):
        edge = at if step_cols[d] < 0 else GRID_B - 1 - at
        return col == edge

    def relay_in(u, d, outbox):
        v = (step_rows[d] + 1) // 2
        return pltpu.make_async_remote_copy(
            src_ref=outbox.at[d, cap - 1],
            dst_ref=relays[u].at[v],
            send_sem=relay_send.at[u, v],
            recv_sem=relay_recv.at[u, v],
            device_id={"section": section, "space": me + step_cols[d]},
            device_id_type=MESH,
        )

    def relay_out(u, d, inbox, recv):
        v = (step_rows[d] + 1) // 2
        return pltpu.make_async_remote_copy(
            src_ref=relays[u].at[v],
            dst_ref=inbox.at[d, cap - 1],
            send_sem=relay_send.at[u, v],
            recv_sem=recv.at[d],
            device_id={"section": section, "space": me + step_rows[d] * GRID_B},
            device_id_type=MESH,
        )

    def direct(d, outbox, inbox, send, recv):
        return pltpu.make_async_remote_copy(
            src_ref=outbox.at[d, pl.ds(0, cap - 1)],
            dst_ref=inbox.at[d, pl.ds(0, cap - 1)],
            send_sem=send.at[d],
            recv_sem=recv.at[d],
            device_id=target(d),
            device_id_type=MESH,
        )

    def relaying(d):
        r = row + step_rows[d]
        return outer(d, 0) & (r >= 0) & (r < grid_a)

    def relay_forward(u, outbox, inbox, send, recv):
        for d in corners:

            @pl.when(relaying(d))
            def _():
                relay_in(u, d, outbox).wait_recv()
                relay_out(u, d, inbox, recv).start()

    def relay_sent(u, outbox, inbox, send, recv):
        for d in corners:

            @pl.when(relaying(d))
            def _():
                relay_out(u, d, inbox, recv).wait_send()

    def halo_start(u, ds, table, outbox, inbox, send, recv):
        for d in ds:

            @pl.when(inside(d, 1))
            def _():
                for j in range(cap):
                    tile = table[rows[j, d]]
                    outbox[d, j] = jnp.where(j < counts[d], tile, jnp.zeros_like(tile))
                if d in corners:

                    @pl.when(outer(d, 1) & (u < 2))
                    def _():
                        relay_in(u, d, outbox).start()
                        direct(d, outbox, inbox, send, recv).start()

                    @pl.when(jnp.logical_not(outer(d, 1) & (u < 2)))
                    def _():
                        halo_copy(d, outbox, inbox, send, recv).start()

                else:
                    halo_copy(d, outbox, inbox, send, recv).start()

    def halo_sent(u, ds, outbox, inbox, send, recv):
        for d in ds:
            if d in corners:

                @pl.when(inside(d, 1) & outer(d, 1) & (u < 2))
                def _():
                    relay_in(u, d, outbox).wait_send()
                    direct(d, outbox, inbox, send, recv).wait_send()

                @pl.when(inside(d, 1) & jnp.logical_not(outer(d, 1) & (u < 2)))
                def _():
                    halo_copy(d, outbox, inbox, send, recv).wait_send()

            else:

                @pl.when(inside(d, 1))
                def _():
                    halo_copy(d, outbox, inbox, send, recv).wait_send()

    def halo_receive(table, outbox, inbox, send, recv):
        for d in range(dirs):
            place = pl.ds(tiles + d * cap, cap)

            @pl.when(inside(d, -1))
            def _():
                halo_copy(d, outbox, inbox, send, recv).wait_recv()
                table[place] = inbox[d]

            @pl.when(jnp.logical_not(inside(d, -1)))
            def _():
                table[place] = jnp.zeros((cap,) + table.shape[1:], table.dtype)

        table[tiles + dirs * cap] = jnp.zeros(table.shape[1:], table.dtype)

    def skip_copy(t):
        return pltpu.make_async_remote_copy(
            src_ref=table2.at[pl.ds(t, 2)],
            dst_ref=table3.at[pl.ds(t, 2)],
            send_sem=send_skip.at[t // 2],
            recv_sem=recv_skip.at[t // 2],
            device_id=sibling,
            device_id_type=MESH,
        )

    halo1 = (outbox1, inbox1, send1, recv1)
    halo2 = (outbox2, inbox2, send2, recv2)
    halo3 = (outbox3, inbox3, send3, recv3)

    for load in loads[:3]:
        load.wait()
    peers = jnp.int32(1)
    for d in range(dirs):
        peers += jnp.where(inside(d, -1), 1, 0).astype(jnp.int32)
    pl.semaphore_wait(barrier, peers)

    halo_start(0, order, table1, *halo1)

    @pl.when(section == 0)
    def _():
        table3[...] = jnp.zeros(table3.shape, table3.dtype)

    for load in loads[4:]:
        load.start()
    relay_forward(0, *halo1)

    loads[3].wait()
    loads[4].wait()
    halo_receive(table1, *halo1)

    def emit_first(t, part):
        part = jnp.maximum(part, 0.0).astype(table2.dtype)
        table2[t] = part[:, :vox]
        table2[t + 1] = part[:, vox:]

        @pl.when(section == 0)
        def _():
            skip_copy(t).start()

    def send_first(i, _):
        d = jnp.int32(order[0])
        for n in range(1, dirs):
            d = jnp.where(i == n, order[n], d)
        step = d + jnp.where(d >= dirs // 2, 1, 0).astype(jnp.int32)
        da, db = step // 3 - 1, step % 3 - 1
        r, c = row + da, col + db

        @pl.when((r >= 0) & (r < grid_a) & (c >= 0) & (c < GRID_B))
        def _():
            part = conv_pair(ids, w1, table1, rows[0, d], rows[1, d])
            part = jnp.maximum(part, 0.0).astype(outbox2.dtype)
            for j in range(cap):
                tile = part[:, j * vox : (j + 1) * vox]
                outbox2[d, j] = jnp.where(j < counts[d], tile, jnp.zeros_like(tile))
            far = {"section": section, "space": me + da * GRID_B + db}
            via = (da != 0) & (((db < 0) & (col == 1)) | ((db > 0) & (col == GRID_B - 2)))
            v = (da + 1) // 2

            @pl.when(via)
            def _():
                pltpu.make_async_remote_copy(
                    src_ref=outbox2.at[d, cap - 1],
                    dst_ref=relay2.at[v],
                    send_sem=relay_send.at[1, v],
                    recv_sem=relay_recv.at[1, v],
                    device_id={"section": section, "space": me + db},
                    device_id_type=MESH,
                ).start()
                pltpu.make_async_remote_copy(
                    src_ref=outbox2.at[d, pl.ds(0, cap - 1)],
                    dst_ref=inbox2.at[d, pl.ds(0, cap - 1)],
                    send_sem=send2.at[d],
                    recv_sem=recv2.at[d],
                    device_id=far,
                    device_id_type=MESH,
                ).start()

            @pl.when(jnp.logical_not(via))
            def _():
                pltpu.make_async_remote_copy(
                    src_ref=outbox2.at[d],
                    dst_ref=inbox2.at[d],
                    send_sem=send2.at[d],
                    recv_sem=recv2.at[d],
                    device_id=far,
                    device_id_type=MESH,
                ).start()

        return 0

    lax.fori_loop(0, dirs, send_first, 0)
    conv_tiles(ids, w1, table1, emit_first, 0, tiles // 2, tiles // 2)
    relay_forward(1, *halo2)
    conv_tiles(ids, w1, table1, emit_first, tiles // 2, tiles, tiles // 2)

    @pl.when(section == 1)
    def _():
        lax.fori_loop(0, tiles // 2, lambda i, _: (skip_copy(2 * i).wait_recv(), 0)[1], 0)
        halo_start(2, order, table3, *halo3)

    for load in loads[5:]:
        load.wait()

    halo_receive(table2, *halo2)

    def emit_out(t, part):
        acc[t // 2] = part
        part = jnp.maximum(part, 0.0).astype(out.dtype)
        out[t] = part[:, :vox]
        out[t + 1] = part[:, vox:]

    conv_tiles(ids, w2, table2, emit_out, 0, tiles, tiles, more=(w3, table3, koff // 2))

    @pl.when(section == 1)
    def _():
        halo_receive(table3, *halo3)

        def emit_sum(t, part):
            part = jnp.maximum(part + acc[t // 2], 0.0).astype(out.dtype)
            out[t] = part[:, :vox]
            out[t + 1] = part[:, vox:]

        conv_tiles(ids, w3, table3, emit_sum, 0, tiles, tiles, outer_offsets)

    @pl.when(section == 0)
    def _():
        lax.fori_loop(0, tiles // 2, lambda i, _: (skip_copy(2 * i).wait_send(), 0)[1], 0)

    @pl.when(section == 1)
    def _():
        halo_sent(2, order, *halo3)

    halo_sent(0, order, *halo1)
    halo_sent(1, order, *halo2)
    relay_sent(0, *halo1)
    relay_sent(1, *halo2)


def local(feats, w_first, w_second, w_skip, send_tiles, send_counts, neighbours):
    ids, send_rows, counts = neighbours[0], send_tiles[0], send_counts[0]
    own = feats[0]
    tiles, channels, vox = own.shape
    dirs, cap = send_rows.shape
    table = pltpu.VMEM((tiles + dirs * cap + 1, channels, vox), own.dtype)
    weights = pltpu.VMEM(w_skip.shape, w_skip.dtype)
    box = pltpu.VMEM((dirs, cap, channels, vox), own.dtype)
    anywhere = pl.BlockSpec(memory_space=pltpu.HBM)
    second = pl.pallas_call(
        network,
        out_shape=pltpu.VMEM((tiles, channels, vox), own.dtype),
        in_specs=[anywhere] * 7,
        out_specs=pl.BlockSpec(memory_space=pltpu.VMEM),
        scratch_shapes=[pltpu.SMEM(a.shape, a.dtype) for a in (ids.T, send_rows.T, counts)]
        + [table] * 3
        + [weights] * 3
        + [pltpu.VMEM((tiles // 2, channels, 2 * vox), jnp.float32)]
        + [box] * 6
        + [pltpu.SemaphoreType.DMA((7,))]
        + [pltpu.SemaphoreType.DMA((dirs,))] * 6
        + [pltpu.SemaphoreType.DMA((tiles // 2,))] * 2
        + [pltpu.VMEM((2, channels, vox), own.dtype)] * 3
        + [pltpu.SemaphoreType.DMA((3, 2))] * 2,
        compiler_params=pltpu.CompilerParams(
            collective_id=0, has_side_effects=True, vmem_limit_bytes=56 * 2**20
        ),
    )(ids.T, send_rows.T, counts, own, w_first[0], w_second[0], w_skip)
    return second[None]


def solution(mesh):
    placed = (
        P("section", "space", None, None),
        P("section", None, None, None),
        P("section", None, None, None),
        P(),
        P("section", "space", None),
        P("section", "space"),
        P("section", None, "space"),
    )
    return jax.shard_map(
        local,
        mesh=mesh,
        in_specs=placed,
        out_specs=P("section", "space", None, None),
        check_vma=False,
    )
```

```python
import jax
import jax.numpy as jnp
from jax import lax
from jax.experimental import pallas as pl
from jax.experimental.pallas import tpu as pltpu
from jax.sharding import PartitionSpec as P

GRID_B = 8

step_rows = (-1, -1, -1, 0, 0, 1, 1, 1)
step_cols = (-1, 0, 1, -1, 1, -1, 0, 1)


def gather_pair(ids, table, k, first, second):
    return jnp.concatenate([table[ids[first, k]], table[ids[second, k]]], axis=1)


def conv_pair(ids, w, table, first, second, offsets=None, more=None):
    offsets = list(range(w.shape[0])) if offsets is None else offsets
    terms = [(w, table, k) for k in offsets] + ([] if more is None else [more])
    acc = None
    for i in range(0, len(terms), 2):
        lhs = [weight[k] for weight, _, k in terms[i : i + 2]]
        rhs = [
            jnp.concatenate([source[first], source[second]], axis=1)
            if more is not None and source is more[1]
            else gather_pair(ids, source, k, first, second)
            for _, source, k in terms[i : i + 2]
        ]
        part = jnp.dot(
            jnp.concatenate(lhs, axis=1),
            jnp.concatenate(rhs, axis=0),
            preferred_element_type=jnp.float32,
        )
        acc = part if acc is None else acc + part
    return acc


def conv_tiles(ids, w, table, emit, begin, end, width, offsets=None, more=None):
    def body(step, _):
        firsts = [begin + step * width + i for i in range(0, width, 2)]
        parts = [conv_pair(ids, w, table, t, t + 1, offsets, more) for t in firsts]
        for t, part in zip(firsts, parts):
            emit(t, part)
        return 0

    if end - begin == width:
        body(0, 0)
    else:
        lax.fori_loop(0, (end - begin) // width, body, 0)


MESH = pl.DeviceIdType.MESH


def network(
    ids_hbm, rows_hbm, counts_hbm, feats, w1_hbm, w2_hbm, w3_hbm, out,
    ids, rows, counts,
    table1, table2, table3, w1, w2, w3, acc,
    outbox1, outbox2, outbox3, inbox1, inbox2, inbox3,
    local_sems, send1, recv1, send2, recv2, send3, recv3, send_skip, recv_skip,
    relay1, relay2, relay3, relay_send, relay_recv,
):
    tiles, _, vox = feats.shape
    cap, dirs = rows.shape
    koff = w1.shape[0]
    outer_offsets = [k for k in range(koff) if k != koff // 2]
    corners = [d for d in range(dirs) if step_rows[d] != 0 and step_cols[d] != 0]
    order = [0, 2, 5, 7, 3, 4, 1, 6]
    relays = (relay1, relay2, relay3)
    section = lax.axis_index("section")
    me = lax.axis_index("space")
    grid_a = lax.axis_size("space") // GRID_B
    row, col = me // GRID_B, me % GRID_B

    def inside(d, sign):
        r, c = row + sign * step_rows[d], col + sign * step_cols[d]
        return (r >= 0) & (r < grid_a) & (c >= 0) & (c < GRID_B)

    def target(d):
        return {"section": section, "space": me + step_rows[d] * GRID_B + step_cols[d]}

    sibling = {"section": 1 - section, "space": me}

    barrier = pltpu.get_barrier_semaphore()
    for d in range(dirs):

        @pl.when(inside(d, 1))
        def _():
            pl.semaphore_signal(barrier, inc=1, device_id=target(d), device_id_type=MESH)

    pl.semaphore_signal(barrier, inc=1, device_id=sibling, device_id_type=MESH)

    loads = [
        pltpu.make_async_copy(src, dst, local_sems.at[i])
        for i, (src, dst) in enumerate(
            [
                (feats, table1.at[pl.ds(0, tiles)]),
                (rows_hbm, rows),
                (counts_hbm, counts),
                (ids_hbm, ids),
                (w1_hbm, w1),
                (w2_hbm, w2),
                (w3_hbm, w3),
            ]
        )
    ]
    for load in loads[:4]:
        load.start()

    def halo_copy(d, outbox, inbox, send, recv):
        return pltpu.make_async_remote_copy(
            src_ref=outbox.at[d],
            dst_ref=inbox.at[d],
            send_sem=send.at[d],
            recv_sem=recv.at[d],
            device_id=target(d),
            device_id_type=MESH,
        )

    def outer(d, at):
        edge = at if step_cols[d] < 0 else GRID_B - 1 - at
        return col == edge

    def relay_in(u, d, outbox):
        v = (step_rows[d] + 1) // 2
        return pltpu.make_async_remote_copy(
            src_ref=outbox.at[d, cap - 1],
            dst_ref=relays[u].at[v],
            send_sem=relay_send.at[u, v],
            recv_sem=relay_recv.at[u, v],
            device_id={"section": section, "space": me + step_cols[d]},
            device_id_type=MESH,
        )

    def relay_out(u, d, inbox, recv):
        v = (step_rows[d] + 1) // 2
        return pltpu.make_async_remote_copy(
            src_ref=relays[u].at[v],
            dst_ref=inbox.at[d, cap - 1],
            send_sem=relay_send.at[u, v],
            recv_sem=recv.at[d],
            device_id={"section": section, "space": me + step_rows[d] * GRID_B},
            device_id_type=MESH,
        )

    def direct(d, outbox, inbox, send, recv):
        return pltpu.make_async_remote_copy(
            src_ref=outbox.at[d, pl.ds(0, cap - 1)],
            dst_ref=inbox.at[d, pl.ds(0, cap - 1)],
            send_sem=send.at[d],
            recv_sem=recv.at[d],
            device_id=target(d),
            device_id_type=MESH,
        )

    def relaying(d):
        r = row + step_rows[d]
        return outer(d, 0) & (r >= 0) & (r < grid_a)

    def relay_forward(u, outbox, inbox, send, recv):
        for d in corners:

            @pl.when(relaying(d))
            def _():
                relay_in(u, d, outbox).wait_recv()
                relay_out(u, d, inbox, recv).start()

    def relay_sent(u, outbox, inbox, send, recv):
        for d in corners:

            @pl.when(relaying(d))
            def _():
                relay_out(u, d, inbox, recv).wait_send()

    def halo_start(u, ds, table, outbox, inbox, send, recv):
        for d in ds:

            @pl.when(inside(d, 1))
            def _():
                for j in range(cap):
                    tile = table[rows[j, d]]
                    outbox[d, j] = jnp.where(j < counts[d], tile, jnp.zeros_like(tile))
                if d in corners:

                    @pl.when(outer(d, 1) & (u < 2))
                    def _():
                        relay_in(u, d, outbox).start()
                        direct(d, outbox, inbox, send, recv).start()

                    @pl.when(jnp.logical_not(outer(d, 1) & (u < 2)))
                    def _():
                        halo_copy(d, outbox, inbox, send, recv).start()

                else:
                    halo_copy(d, outbox, inbox, send, recv).start()

    def halo_sent(u, ds, outbox, inbox, send, recv):
        for d in ds:
            if d in corners:

                @pl.when(inside(d, 1) & outer(d, 1) & (u < 2))
                def _():
                    relay_in(u, d, outbox).wait_send()
                    direct(d, outbox, inbox, send, recv).wait_send()

                @pl.when(inside(d, 1) & jnp.logical_not(outer(d, 1) & (u < 2)))
                def _():
                    halo_copy(d, outbox, inbox, send, recv).wait_send()

            else:

                @pl.when(inside(d, 1))
                def _():
                    halo_copy(d, outbox, inbox, send, recv).wait_send()

    def halo_receive(table, outbox, inbox, send, recv):
        for d in range(dirs):
            place = pl.ds(tiles + d * cap, cap)

            @pl.when(inside(d, -1))
            def _():
                halo_copy(d, outbox, inbox, send, recv).wait_recv()
                table[place] = inbox[d]

            @pl.when(jnp.logical_not(inside(d, -1)))
            def _():
                table[place] = jnp.zeros((cap,) + table.shape[1:], table.dtype)

        table[tiles + dirs * cap] = jnp.zeros(table.shape[1:], table.dtype)

    def skip_copy(t):
        return pltpu.make_async_remote_copy(
            src_ref=table2.at[pl.ds(t, 2)],
            dst_ref=table3.at[pl.ds(t, 2)],
            send_sem=send_skip.at[t // 2],
            recv_sem=recv_skip.at[t // 2],
            device_id=sibling,
            device_id_type=MESH,
        )

    halo1 = (outbox1, inbox1, send1, recv1)
    halo2 = (outbox2, inbox2, send2, recv2)
    halo3 = (outbox3, inbox3, send3, recv3)

    for load in loads[:3]:
        load.wait()
    peers = jnp.int32(1)
    for d in range(dirs):
        peers += jnp.where(inside(d, -1), 1, 0).astype(jnp.int32)
    pl.semaphore_wait(barrier, peers)

    halo_start(0, order, table1, *halo1)

    @pl.when(section == 0)
    def _():
        table3[...] = jnp.zeros(table3.shape, table3.dtype)

    for load in loads[4:]:
        load.start()
    relay_forward(0, *halo1)

    loads[3].wait()
    loads[4].wait()
    halo_receive(table1, *halo1)

    def emit_first(t, part):
        part = jnp.maximum(part, 0.0).astype(table2.dtype)
        table2[t] = part[:, :vox]
        table2[t + 1] = part[:, vox:]

        @pl.when(section == 0)
        def _():
            skip_copy(t).start()

    def send_first(i, _):
        d = jnp.int32(order[0])
        for n in range(1, dirs):
            d = jnp.where(i == n, order[n], d)
        step = d + jnp.where(d >= dirs // 2, 1, 0).astype(jnp.int32)
        da, db = step // 3 - 1, step % 3 - 1
        r, c = row + da, col + db

        @pl.when((r >= 0) & (r < grid_a) & (c >= 0) & (c < GRID_B))
        def _():
            part = conv_pair(ids, w1, table1, rows[0, d], rows[1, d])
            part = jnp.maximum(part, 0.0).astype(outbox2.dtype)
            for j in range(cap):
                tile = part[:, j * vox : (j + 1) * vox]
                outbox2[d, j] = jnp.where(j < counts[d], tile, jnp.zeros_like(tile))
            far = {"section": section, "space": me + da * GRID_B + db}
            via = (da != 0) & (((db < 0) & (col == 1)) | ((db > 0) & (col == GRID_B - 2)))
            v = (da + 1) // 2

            @pl.when(via)
            def _():
                pltpu.make_async_remote_copy(
                    src_ref=outbox2.at[d, cap - 1],
                    dst_ref=relay2.at[v],
                    send_sem=relay_send.at[1, v],
                    recv_sem=relay_recv.at[1, v],
                    device_id={"section": section, "space": me + db},
                    device_id_type=MESH,
                ).start()
                pltpu.make_async_remote_copy(
                    src_ref=outbox2.at[d, pl.ds(0, cap - 1)],
                    dst_ref=inbox2.at[d, pl.ds(0, cap - 1)],
                    send_sem=send2.at[d],
                    recv_sem=recv2.at[d],
                    device_id=far,
                    device_id_type=MESH,
                ).start()

            @pl.when(jnp.logical_not(via))
            def _():
                pltpu.make_async_remote_copy(
                    src_ref=outbox2.at[d],
                    dst_ref=inbox2.at[d],
                    send_sem=send2.at[d],
                    recv_sem=recv2.at[d],
                    device_id=far,
                    device_id_type=MESH,
                ).start()

        return 0

    lax.fori_loop(0, dirs, send_first, 0)
    conv_tiles(ids, w1, table1, emit_first, 0, tiles // 2, tiles // 2)
    relay_forward(1, *halo2)
    conv_tiles(ids, w1, table1, emit_first, tiles // 2, tiles, tiles // 2)

    @pl.when(section == 1)
    def _():
        lax.fori_loop(0, tiles // 2, lambda i, _: (skip_copy(2 * i).wait_recv(), 0)[1], 0)
        halo_start(2, [0, 2, 5, 7, 1, 6, 3, 4], table3, *halo3)

    for load in loads[5:]:
        load.wait()

    halo_receive(table2, *halo2)

    def emit_out(t, part):
        acc[t // 2] = part
        part = jnp.maximum(part, 0.0).astype(out.dtype)
        out[t] = part[:, :vox]
        out[t + 1] = part[:, vox:]

    conv_tiles(ids, w2, table2, emit_out, 0, tiles, tiles, more=(w3, table3, koff // 2))

    @pl.when(section == 1)
    def _():
        halo_receive(table3, *halo3)

        def emit_sum(t, part):
            part = jnp.maximum(part + acc[t // 2], 0.0).astype(out.dtype)
            out[t] = part[:, :vox]
            out[t + 1] = part[:, vox:]

        conv_tiles(ids, w3, table3, emit_sum, 0, tiles, tiles, outer_offsets)

    @pl.when(section == 0)
    def _():
        lax.fori_loop(0, tiles // 2, lambda i, _: (skip_copy(2 * i).wait_send(), 0)[1], 0)

    @pl.when(section == 1)
    def _():
        halo_sent(2, order, *halo3)

    halo_sent(0, order, *halo1)
    halo_sent(1, order, *halo2)
    relay_sent(0, *halo1)
    relay_sent(1, *halo2)


def write_out(tiles_vmem, out, sems):
    parts = sems.shape[0]
    size = out.shape[0] // parts
    copies = [
        pltpu.make_async_copy(
            tiles_vmem.at[pl.ds(i * size, size)], out.at[pl.ds(i * size, size)], sems.at[i]
        )
        for i in range(parts)
    ]
    for copy in copies:
        copy.start()
    for copy in copies:
        copy.wait()


def local(feats, w_first, w_second, w_skip, send_tiles, send_counts, neighbours):
    ids, send_rows, counts = neighbours[0], send_tiles[0], send_counts[0]
    own = feats[0]
    tiles, channels, vox = own.shape
    dirs, cap = send_rows.shape
    table = pltpu.VMEM((tiles + dirs * cap + 1, channels, vox), own.dtype)
    weights = pltpu.VMEM(w_skip.shape, w_skip.dtype)
    box = pltpu.VMEM((dirs, cap, channels, vox), own.dtype)
    anywhere = pl.BlockSpec(memory_space=pltpu.HBM)
    second = pl.pallas_call(
        network,
        out_shape=pltpu.VMEM((tiles, channels, vox), own.dtype),
        in_specs=[anywhere] * 7,
        out_specs=pl.BlockSpec(memory_space=pltpu.VMEM),
        scratch_shapes=[pltpu.SMEM(a.shape, a.dtype) for a in (ids.T, send_rows.T, counts)]
        + [table] * 3
        + [weights] * 3
        + [pltpu.VMEM((tiles // 2, channels, 2 * vox), jnp.float32)]
        + [box] * 6
        + [pltpu.SemaphoreType.DMA((7,))]
        + [pltpu.SemaphoreType.DMA((dirs,))] * 6
        + [pltpu.SemaphoreType.DMA((tiles // 2,))] * 2
        + [pltpu.VMEM((2, channels, vox), own.dtype)] * 3
        + [pltpu.SemaphoreType.DMA((3, 2))] * 2,
        compiler_params=pltpu.CompilerParams(
            collective_id=0, has_side_effects=True, vmem_limit_bytes=56 * 2**20
        ),
    )(ids.T, send_rows.T, counts, own, w_first[0], w_second[0], w_skip)
    second = pltpu.with_memory_space_constraint(second, pltpu.VMEM)
    written = pl.pallas_call(
        write_out,
        out_shape=jax.ShapeDtypeStruct(second.shape, second.dtype),
        in_specs=[pl.BlockSpec(memory_space=pltpu.VMEM)],
        out_specs=pl.BlockSpec(memory_space=pltpu.HBM),
        scratch_shapes=[pltpu.SemaphoreType.DMA((4,))],
    )(second)
    return written[None]


def solution(mesh):
    placed = (
        P("section", "space", None, None),
        P("section", None, None, None),
        P("section", None, None, None),
        P(),
        P("section", "space", None),
        P("section", "space"),
        P("section", None, "space"),
    )
    return jax.shard_map(
        local,
        mesh=mesh,
        in_specs=placed,
        out_specs=P("section", "space", None, None),
        check_vma=False,
    )
```
